32 devices in a mesh: gx: 2 (over core), gy: 4 (over z), gz: 4 (over y, x).
Axes of the slice: x: 2, y: 2, z: 4, core: 2. Of those that a mesh axis runs over, the one named last changes fastest.
Arguments:
- head_old: float32 [256, 16, 512], P('gz', 'gx', 'gy'), may hold values from -0.5 to -0.05
- ks_scale: float32 [256, 16, 512], P('gz', 'gx', 'gy'), may hold values from 0.5 to 2
- soil_class: int32 [256, 16, 512], P('gz', 'gx', 'gy'), may hold values from 0 to 5
- emitter_cells: int32 [2, 4, 256], P('gx', 'gy'), may hold values from 0 to 1023
Outputs:
- head: float32 [256, 16, 512], P('gz', 'gx', 'gy')
- water: float32 [256, 16, 512], P('gz', 'gx', 'gy')
The draws below stay inside these ranges and needn't reach their ends.
All inputs are finite; a program needn't handle non-finite values.
Results may differ from the reference program's by a relative error of at most 0.0003.
Values sent between devices are 32-bit elements; how exact they have to be, the bound alone decides.
No kernel may reach another device: no remote copies, remote signals or barrier semaphores. Data moves between devices by JAX's collectives and lax.ppermute only.
A program may use at most 64 MiB of HBM per device.

```python
import math
import jax
import jax.numpy as jnp
from jax import lax

CX = 8
CY = 128
EMIT = 256
ITERS = 2
DRIP = 30
CLASSES = 6
NX = 16
NY = 512
NZ = 256
BLOCKS_X = 2
BLOCKS_Y = 4


def touch_ends(result, own_key, least, top_value):
    extent = result.shape
    index_at = [jax.random.randint(jax.random.fold_in(own_key, axis), (), 0, extent[axis]) for axis in range(len(extent))]
    result = result.at[tuple(index_at)].set(least)
    longest = extent.index(max(extent))
    index_at[longest] = (index_at[longest] + 1) % extent[longest]
    return result.at[tuple(index_at)].set(top_value)


def level_of(key, shape, pieces, low, high):
    level = 1.0
    for dim, blocks in pieces:
        steps = jax.random.uniform(jax.random.fold_in(jax.random.fold_in(key, 6), dim), (blocks,), jnp.float32, low / len(pieces), high / len(pieces))
        level = level * jnp.repeat(jnp.exp(steps), shape[dim] // blocks).reshape((-1,) + (1,) * (len(shape) - 1 - dim))
    return level


def setup_inputs(seed: int = 0) -> dict:
    seeds = jax.random.split(jax.random.key(seed), 5)
    return {
        "head_old": jnp.clip(-0.5 + 0.45 * jax.random.uniform(seeds[0], (NZ, NX, NY), jnp.float32) ** level_of(seeds[0], (NZ, NX, NY), ((0, 4), (1, 2), (2, 4)), -0.2, 0.2), -0.5, -0.05),
        "ks_scale": jnp.clip(jnp.exp(math.log(2.0) - 1.3862944 * jax.random.uniform(seeds[1], (NZ, NX, NY), jnp.float32) ** level_of(seeds[1], (NZ, NX, NY), ((0, 4), (1, 2), (2, 4)), -0.2, 0.2)), 0.5, 2.0),
        "soil_class": touch_ends(jax.random.randint(seeds[2], (NZ, NX, NY), 0, CLASSES), jax.random.fold_in(seeds[2], 1), 0, CLASSES - 1).astype(jnp.int32),
        "emitter_cells": touch_ends(jax.random.randint(seeds[3], (BLOCKS_X, BLOCKS_Y, EMIT), 0, CX * CY), jax.random.fold_in(seeds[3], 1), 0, (CX * CY) - 1).astype(jnp.int32),
    }


ALPHA_TABLE = (3.6, 2.0, 1.9, 1.0, 5.9, 1.6)
SHAPE_TABLE = (1.56, 1.41, 1.31, 1.23, 1.48, 1.37)
RESIDUAL_TABLE = (0.078, 0.067, 0.095, 0.089, 0.1, 0.034)
SATURATED_TABLE = (0.43, 0.45, 0.41, 0.43, 0.39, 0.46)
CONDUCT_TABLE = (0.2496, 0.108, 0.0624, 0.0168, 0.3144, 0.06)
layer_height = 0.01
column_width = 2.0
time_step = 2.0
storage_floor = 0.001
emitter_flow = 0.096
vertical_gain = 1.0 / (layer_height * layer_height)
gravity_gain = 1.0 / layer_height
lateral_gain = 1.0 / (column_width * column_width)
storage_gain = 1.0 / time_step
emitter_rate = emitter_flow / (column_width * column_width * layer_height)

def soil_params(soil_class, ks_scale):
    air_entry = jnp.zeros(soil_class.shape, jnp.float32)
    shape_n = air_entry
    theta_res = air_entry
    theta_sat = air_entry
    sat_conduct = air_entry
    for number in range(len(ALPHA_TABLE)):
        chosen = soil_class == number
        air_entry = jnp.where(chosen, ALPHA_TABLE[number], air_entry)
        shape_n = jnp.where(chosen, SHAPE_TABLE[number], shape_n)
        theta_res = jnp.where(chosen, RESIDUAL_TABLE[number], theta_res)
        theta_sat = jnp.where(chosen, SATURATED_TABLE[number], theta_sat)
        sat_conduct = jnp.where(chosen, CONDUCT_TABLE[number], sat_conduct)
    return (air_entry, shape_n, theta_res, theta_sat, sat_conduct * ks_scale)

def effective_state(pressure, air_entry, shape_n):
    shape_m = 1.0 - 1.0 / shape_n
    scaled = air_entry * jnp.abs(pressure)
    lifted = 1.0 + scaled ** shape_n
    effective = jnp.where(pressure < 0.0, lifted ** (-shape_m), 1.0)
    return (effective, scaled, lifted, shape_m)

def flow_factor(effective, shape_m, sat_conduct):
    inner_term = 1.0 - (1.0 - effective ** (1.0 / shape_m)) ** shape_m
    return sat_conduct * jnp.sqrt(effective) * inner_term * inner_term

def retention(pressure, air_entry, shape_n, theta_res, theta_sat, sat_conduct):
    effective, scaled, lifted, shape_m = effective_state(pressure, air_entry, shape_n)
    spread = theta_sat - theta_res
    moisture = theta_res + spread * effective
    capacity_core = jnp.where(pressure < 0.0, spread * air_entry * shape_n * shape_m * scaled ** (shape_n - 1.0) * lifted ** (-shape_m - 1.0), 0.0)
    return (moisture, flow_factor(effective, shape_m, sat_conduct), capacity_core + storage_floor)

def assemble(z_face, z_head, x_face, x_head, y_face, y_head, moisture, capacity, theta_old, source):
    z_flux = z_face * ((z_head[:-1] - z_head[1:]) * vertical_gain + gravity_gain)
    x_flux = x_face * (x_head[:, :-1] - x_head[:, 1:]) * lateral_gain
    y_flux = y_face * (y_head[:, :, :-1] - y_head[:, :, 1:]) * lateral_gain
    residual = (moisture - theta_old) * storage_gain + (z_flux[1:] - z_flux[:-1]) + (x_flux[:, 1:] - x_flux[:, :-1]) + (y_flux[:, :, 1:] - y_flux[:, :, :-1]) - source
    z_gain = z_face * vertical_gain
    diagonal = capacity * storage_gain + (z_gain[:-1] + z_gain[1:]) + (x_face[:, 1:] + x_face[:, :-1]) * lateral_gain + (y_face[:, :, 1:] + y_face[:, :, :-1]) * lateral_gain
    return (-z_gain[:-1], diagonal, -z_gain[1:], -residual)

def thomas(lower, diagonal, upper, right_side):

    def forward(carried, entries):
        ratio_prev, shift_prev = carried
        sub_entry, diag_entry, super_entry, rhs_entry = entries
        pivot = diag_entry - sub_entry * ratio_prev
        ratio_new = super_entry / pivot
        shift_new = (rhs_entry - sub_entry * shift_prev) / pivot
        return ((ratio_new, shift_new), (ratio_new, shift_new))
    zeros_plane = jnp.zeros_like(diagonal[0])
    unused, (ratios, shifts) = lax.scan(forward, (zeros_plane, zeros_plane), (lower, diagonal, upper, right_side))

    def backward(value_next, entries):
        ratio_here, shift_here = entries
        value = shift_here - ratio_here * value_next
        return (value, value)
    unused_last, values = lax.scan(backward, zeros_plane, (ratios, shifts), reverse=True)
    return values

def reference(head_old, ks_scale, soil_class, emitter_cells):
    air_entry, shape_n, theta_res, theta_sat, sat_conduct = soil_params(soil_class, ks_scale)
    theta_old, unused_k, unused_c = retention(head_old, air_entry, shape_n, theta_res, theta_sat, sat_conduct)
    block_row = jnp.arange(BLOCKS_X, dtype=jnp.int32)[:, None, None] * CX
    block_col = jnp.arange(BLOCKS_Y, dtype=jnp.int32)[None, :, None] * CY
    row_index = (block_row + emitter_cells // CY).reshape(-1).astype(jnp.int32)
    col_index = (block_col + emitter_cells % CY).reshape(-1).astype(jnp.int32)
    plane = jnp.zeros((NX, NY), jnp.float32).at[row_index, col_index].add(emitter_rate)
    source = jnp.zeros((NZ, NX, NY), jnp.float32).at[DRIP].set(plane)
    pressure = head_old
    for iteration in range(ITERS):
        moisture, conductivity, capacity = retention(pressure, air_entry, shape_n, theta_res, theta_sat, sat_conduct)
        zero_layer = jnp.zeros_like(pressure[:1])
        z_face = jnp.concatenate([zero_layer, 0.5 * (conductivity[:-1] + conductivity[1:]), conductivity[-1:]], axis=0)
        z_head = jnp.concatenate([zero_layer, pressure, zero_layer], axis=0)
        zero_row = jnp.zeros_like(pressure[:, :1])
        x_face = jnp.concatenate([zero_row, 0.5 * (conductivity[:, :-1] + conductivity[:, 1:]), zero_row], axis=1)
        x_head = jnp.concatenate([zero_row, pressure, zero_row], axis=1)
        zero_col = jnp.zeros_like(pressure[:, :, :1])
        y_face = jnp.concatenate([zero_col, 0.5 * (conductivity[:, :, :-1] + conductivity[:, :, 1:]), zero_col], axis=2)
        y_head = jnp.concatenate([zero_col, pressure, zero_col], axis=2)
        lower, diagonal, upper, right_side = assemble(z_face, z_head, x_face, x_head, y_face, y_head, moisture, capacity, theta_old, source)
        pressure = pressure + thomas(lower, diagonal, upper, right_side)
    water, unused_k2, unused_c2 = retention(pressure, air_entry, shape_n, theta_res, theta_sat, sat_conduct)
    return (pressure, water)
```

```python
import functools

import jax
import jax.numpy as jnp
from jax import lax
from jax.experimental import pallas as pl
from jax.experimental.pallas import tpu as pltpu
from jax.sharding import PartitionSpec as P

DRIP = 30

ALPHA_TABLE = (3.6, 2.0, 1.9, 1.0, 5.9, 1.6)
SHAPE_TABLE = (1.56, 1.41, 1.31, 1.23, 1.48, 1.37)
RESIDUAL_TABLE = (0.078, 0.067, 0.095, 0.089, 0.1, 0.034)
SATURATED_TABLE = (0.43, 0.45, 0.41, 0.43, 0.39, 0.46)
CONDUCT_TABLE = (0.2496, 0.108, 0.0624, 0.0168, 0.3144, 0.06)
layer_height = 0.01
column_width = 2.0
time_step = 2.0
storage_floor = 0.001
emitter_flow = 0.096
vertical_gain = 1.0 / (layer_height * layer_height)
gravity_gain = 1.0 / layer_height
lateral_gain = 1.0 / (column_width * column_width)
storage_gain = 1.0 / time_step
emitter_rate = emitter_flow / (column_width * column_width * layer_height)

POWER_TABLE = tuple(n - 1.0 for n in SHAPE_TABLE)
M_TABLE = tuple(1.0 - 1.0 / n for n in SHAPE_TABLE)
SPREAD_TABLE = tuple(s - r for s, r in zip(SATURATED_TABLE, RESIDUAL_TABLE))
CAP_TABLE = tuple(
    storage_gain * s * a * p for s, a, p in zip(SPREAD_TABLE, ALPHA_TABLE, POWER_TABLE)
)
floor_gain = storage_floor * storage_gain
half_lateral = 0.5 * lateral_gain

ROWS, LANES = 8, 128
F32 = jnp.float32
SLOT = 40
PLANES = 9
SIDE = 2
PACK = -(-(PLANES * (ROWS + SIDE)) // ROWS) * ROWS
UNROLL = 4


def roll(value, shift, axis=1):
    size = value.shape[axis]
    shift = shift % size
    return value if shift == 0 else pltpu.roll(value, shift, axis)


def tile(z):
    return pl.ds(pl.multiple_of(z * ROWS, ROWS), ROWS)


def line(row, count):
    return pl.ds(row, count, stride=ROWS)


def iota(shape, dim):
    return lax.broadcasted_iota(jnp.int32, shape, dim)


def look_up(kinds, *tables):
    chosen = [kinds == float(number) for number in range(1, len(ALPHA_TABLE))]
    found = []
    for table in tables:
        value = jnp.full(kinds.shape, table[0], F32)
        for number, mask in enumerate(chosen, 1):
            value = jnp.where(mask, table[number], value)
        found.append(value)
    return found


def retention(head, alpha, power, m_shape, conduct):
    wet = head >= 0.0
    scaled = alpha * jnp.abs(head)
    raised = jnp.where(wet, 0.0, jnp.exp(power * jnp.log(scaled)))
    lifted = 1.0 + raised * scaled
    root = jnp.exp((-0.5 * m_shape) * jnp.log(lifted))
    effective = root * root
    product = raised * effective
    inner = 1.0 - product
    return conduct * root * inner * inner, effective, product / lifted


def saturation(head, alpha, power, m_shape):
    wet = head >= 0.0
    scaled = alpha * jnp.abs(head)
    raised = jnp.where(wet, 0.0, jnp.exp(power * jnp.log(scaled)))
    return jnp.exp(-m_shape * jnp.log(1.0 + raised * scaled))


def raw_retention(head, scale, kinds):
    alpha, power, m_shape, conduct, cap = look_up(
        kinds, ALPHA_TABLE, POWER_TABLE, M_TABLE, CONDUCT_TABLE, CAP_TABLE
    )
    k_value, unused, shape = retention(head, alpha, power, m_shape, conduct * scale)
    return k_value, cap * shape + floor_gain


def each_layer(count, body, carry):
    step = UNROLL if count % UNROLL == 0 else 1

    def several(chunk, carry):
        for inner in range(step):
            carry = body(chunk * step + inner, carry)
        return carry

    return lax.fori_loop(0, count // step, several, carry)


def vertical(z, count, k_ref, h_ref, above):
    below = jnp.minimum(z + 1, count - 1)
    inside = jnp.where(z < count - 1, 0.5, 0.0)
    face = inside * (k_ref[tile(z), :] + k_ref[tile(below), :])
    flux = face * ((h_ref[tile(z), :] - h_ref[tile(below), :]) * vertical_gain + gravity_gain)
    return face * vertical_gain, above - flux, flux


def inner_lateral(k_here, h_here):
    gain = jnp.zeros_like(k_here)
    inflow = jnp.zeros_like(k_here)
    for axis, size in ((0, ROWS), (1, LANES)):
        inside = jnp.where(iota(k_here.shape, axis) < size - 1, half_lateral, 0.0)
        face = inside * (k_here + roll(k_here, -1, axis))
        flux = face * (h_here - roll(h_here, -1, axis))
        gain = gain + face + roll(face, 1, axis)
        inflow = inflow - flux + roll(flux, 1, axis)
    return gain, inflow


def edge_weights(gx, gy, y_count):
    row, lane = iota((ROWS, LANES), 0), iota((ROWS, LANES), 1)
    x_side = row == jnp.where(gx == 0, ROWS - 1, 0)
    west = jnp.where(gy > 0, 0, -1)
    east = jnp.where(gy < y_count - 1, LANES - 1, -1)
    y_side = (lane == west) | (lane == east)
    return jnp.where(x_side, half_lateral, 0.0), jnp.where(y_side, half_lateral, 0.0)


def edge_terms(z, k_here, h_here, weights, side_refs):
    x_k, x_h, y_k, y_h = side_refs
    x_weight, y_weight = weights
    x_face = x_weight * (k_here + x_k[pl.ds(z, 1), :])
    y_face = y_weight * (k_here + y_k[tile(z), :])
    inflow = x_face * (x_h[pl.ds(z, 1), :] - h_here) + y_face * (y_h[tile(z), :] - h_here)
    return x_face + y_face, inflow


def spread_columns(packed, out_ref, count):
    j = iota(packed.shape, 1) & 3
    swapped = jnp.where(j == 2, roll(packed, 1), roll(packed, -1))
    for x in range(ROWS):
        out_ref[line(x, count), :] = roll(swapped, -(4 * (x + 1) + 2))


def eliminations(count):
    order, nodes = [], list(range(count))
    while len(nodes) > 2:
        gone = set()
        for place in range(1, len(nodes) - 1, 2):
            order.append((nodes[place], nodes[place - 1], nodes[place + 1], place == 1))
            gone.add(nodes[place])
        nodes = [node for node in nodes if node not in gone]
    return order


def at(node):
    return slice(node * ROWS, (node + 1) * ROWS)


def reduce_block(count, streams):
    order = eliminations(count)
    carried = [None] * len(streams)
    for place, (j, i, k, opening) in enumerate(order):
        closing = place + 1 == len(order) or order[place + 1][3]
        for s, (e, r, g, t_up, t_down, w) in enumerate(streams):
            e_j, r_j, g_up, g_down = e[at(j), :], r[at(j), :], g[at(i), :], g[at(j), :]
            inverse = 1.0 / (e_j + (g_up + g_down))
            up, down = g_up * inverse, g_down * inverse
            t_up[at(j), :] = up
            t_down[at(j), :] = down
            w[at(j), :] = r_j * inverse
            e_i, r_i = e[at(i), :] + up * e_j, r[at(i), :] + up * r_j
            if not opening:
                e_i, r_i = e_i + carried[s][0], r_i + carried[s][1]
            e[at(i), :] = e_i
            r[at(i), :] = r_i
            g[at(i), :] = g_up * down
            carried[s] = (down * e_j, down * r_j)
            if closing:
                e[at(k), :] = e[at(k), :] + carried[s][0]
                r[at(k), :] = r[at(k), :] + carried[s][1]


def substitute_block(count, streams):
    for j, i, k, unused in reversed(eliminations(count)):
        for x, t_up, t_down, w in streams:
            x[at(j), :] = w[at(j), :] + t_up[at(j), :] * x[at(i), :] + t_down[at(j), :] * x[at(k), :]


def write_port(count, out_ref, e, r, g, k, h, rows, start, is_bottom):
    first, last = slice(0, rows), slice((count - 1) * ROWS, (count - 1) * ROWS + rows)
    open_face = jnp.where(is_bottom, 1.0, 0.0) * k[last, :]
    port = (
        e[first, :],
        e[last, :] + open_face * vertical_gain,
        g[first, :],
        r[first, :],
        r[last, :] - open_face * (h[last, :] * vertical_gain + gravity_gain),
        k[first, :],
        k[last, :],
        h[first, :],
        h[last, :],
    )
    for place, value in enumerate(port):
        out_ref[start + place * rows : start + (place + 1) * rows, :] = value


def solve_chain(blocks, gathered, rows, start):
    def port(block, place):
        low = block * PACK + start + place * rows
        return gathered[low : low + rows, :]

    e, r, links = [], [], []
    for block in range(blocks):
        e += [port(block, 0), port(block, 1)]
        r += [port(block, 3), port(block, 4)]
        links.append(port(block, 2))
        if block < blocks - 1:
            face = 0.5 * (port(block, 6) + port(block + 1, 5))
            flux = face * ((port(block, 8) - port(block + 1, 7)) * vertical_gain + gravity_gain)
            links.append(face * vertical_gain)
            r[-1] = r[-1] - flux
            links_flux = flux
        if block > 0:
            r[-2] = r[-2] + previous
        previous = links_flux if block < blocks - 1 else None
    count = 2 * blocks
    middle = count // 2
    steps = {}

    def fold(node, target, link):
        inverse = 1.0 / (e[node] + link)
        share = link * inverse
        e[target] = e[target] + share * e[node]
        r[target] = r[target] + share * r[node]
        steps[node] = (target, share, r[node] * inverse)

    for step in range(middle):
        fold(step, step + 1, links[step])
        if count - 1 - step > middle:
            fold(count - 1 - step, count - 2 - step, links[count - 2 - step])
    found = {middle: r[middle] / e[middle]}
    for step in range(middle):
        for node in (middle - 1 - step, middle + 1 + step):
            if node in steps:
                target, share, rest = steps[node]
                found[node] = rest + share * found[target]
    return [found[node] for node in range(count)]


def gather_ports(gz, blocks, own, received, gathered):
    for offset, part in enumerate((own, *received)):
        gathered[pl.ds(pl.multiple_of((gz ^ offset) * PACK, ROWS), PACK), :] = part[...]


def own_ends(gz, blocks, found, rows, ends_ref):
    for block in range(blocks):
        ends_ref[block * 2 * ROWS : block * 2 * ROWS + rows, :] = found[2 * block]
        ends_ref[(block * 2 + 1) * ROWS : (block * 2 + 1) * ROWS + rows, :] = found[2 * block + 1]
    return ends_ref[tile(gz * 2), :], ends_ref[tile(gz * 2 + 1), :]


def pack_kernel(h, ks, kinds, cells, columns, rows_out, counts, kind_f):
    gx = lax.axis_index("gx")
    size = h.shape[0]
    count = size // ROWS
    spots = cells[...]
    emitters = spots.shape[1]
    in_row = jnp.where(iota((ROWS, emitters), 0) == (spots >> 7), 1.0, 0.0)
    in_lane = jnp.where(iota((LANES, emitters), 0) == (spots & (LANES - 1)), 1.0, 0.0)
    plane = lax.dot_general(
        in_row.astype(jnp.bfloat16),
        in_lane.astype(jnp.bfloat16),
        (((1,), (1,)), ((), ())),
        preferred_element_type=F32,
    )
    counts[...] = plane
    kind_f[...] = kinds[...].astype(F32)
    group = iota((count, LANES), 1) >> 2
    packed = jnp.zeros((count, LANES), F32)
    for place, source in enumerate((h, ks, kind_f)):
        for x in range(ROWS):
            slot = x + 1 + place * (SLOT // 4)
            moved = roll(source[line(x, count), :], 4 * slot + 2)
            packed = jnp.where(group == slot, moved, packed)
    columns[0:count, :] = packed
    group8 = iota((1, LANES), 1) >> 2
    spot_row = jnp.zeros((1, LANES), F32)
    for x in range(ROWS):
        spot_row = jnp.where(group8 == x + 1, roll(counts[x : x + 1, :], 4 * (x + 1) + 2), spot_row)
    columns[count : count + ROWS, :] = jnp.broadcast_to(spot_row, (ROWS, LANES))
    low = gx == 0
    for place, source in enumerate((h, ks, kind_f)):
        for depth in range(2):
            picked = jnp.where(
                low, source[line(ROWS - 1 - depth, count), :], source[line(depth, count), :]
            )
            start = (2 * place + depth) * count
            rows_out[start : start + count, :] = picked
    edge = jnp.where(low, counts[ROWS - 1 : ROWS, :], counts[0:1, :])
    rows_out[6 * count : 6 * count + ROWS, :] = jnp.broadcast_to(edge, (ROWS, LANES))


def local_kernel(h, ks, kinds, counts, k_out, e_out, r_out, g_out, se_out, alpha_out, power_out, m_out, spread_out, conduct_out):
    count = h.shape[0] // ROWS
    is_top = lax.axis_index("gz") == 0

    def first(z, unused):
        head = h[tile(z), :]
        alpha, power, m_shape, spread, conduct, cap = look_up(
            kinds[tile(z), :].astype(F32), ALPHA_TABLE, POWER_TABLE, M_TABLE, SPREAD_TABLE, CONDUCT_TABLE, CAP_TABLE
        )
        conduct = conduct * ks[tile(z), :]
        k_value, effective, shape = retention(head, alpha, power, m_shape, conduct)
        k_out[tile(z), :] = k_value
        e_out[tile(z), :] = cap * shape + floor_gain
        se_out[tile(z), :] = effective
        alpha_out[tile(z), :] = alpha
        power_out[tile(z), :] = power
        m_out[tile(z), :] = m_shape
        spread_out[tile(z), :] = spread
        conduct_out[tile(z), :] = conduct
        return unused

    each_layer(count, first, 0)
    source = jnp.where(is_top, emitter_rate, 0.0) * counts[...]

    def second(z, above):
        link, inflow, flux = vertical(z, count, k_out, h, above)
        gain, sideways = inner_lateral(k_out[tile(z), :], h[tile(z), :])
        g_out[tile(z), :] = link
        e_out[tile(z), :] = e_out[tile(z), :] + gain
        r_out[tile(z), :] = inflow + sideways
        return flux

    each_layer(count, second, jnp.zeros((ROWS, LANES), F32))
    r_out[at(DRIP), :] = r_out[at(DRIP), :] + source


def merge_halo(gx, gy, from_even, from_odd, far_even, far_odd):
    lane = iota(from_even.shape, 1)
    even = (gy & 1) == 0
    j = lane & 3

    def both(e_part, o_part):
        left = jnp.where(even, o_part[...], e_part[...])
        right = jnp.where(even, e_part[...], o_part[...])
        return jnp.where(j < 2, left, right)

    near, far = both(from_even, from_odd), both(far_even, far_odd)
    low = gx == 0
    corner = jnp.where(low, 9, 0)
    group = lane >> 2
    hit = (group == corner) | (group == corner + SLOT // 4) | (group == corner + SLOT // 2)
    return jnp.where(hit, jnp.where(low, roll(far, 32), roll(far, -32)), near)


def unpack(packed):
    used = iota(packed.shape, 1) < SLOT
    return [jnp.where(used, roll(packed, -SLOT * place), 0.0) for place in range(3)]


def side_lateral(gx, gy, y_count, near_k, near_h, row1, row2, col, own):
    lane = iota(near_k.shape, 1)
    low = gx == 0

    def pair(here, there, weight):
        face = weight * (here[0] + there[0])
        return face, face * (there[1] - here[1])

    def moved(cells, shift):
        return [roll(part, shift) for part in cells]

    def pick(mask, yes, no):
        return [jnp.where(mask, a, b) for a, b in zip(yes, no)]

    corner_west = pick(low, moved(col, -37), moved(col, -1))
    corner_east = pick(low, moved(col, LANES - 1 - 38), moved(col, LANES - 1 - 2))
    west = pick(lane == 0, corner_west, moved(row1, 1))
    east = pick(lane == LANES - 1, corner_east, moved(row1, -1))
    west_weight = jnp.where((lane > 0) | (gy > 0), half_lateral, 0.0)
    east_weight = jnp.where((lane < LANES - 1) | (gy < y_count - 1), half_lateral, 0.0)
    row_terms = [
        pair(row1, (near_k, near_h), half_lateral),
        pair(row1, row2, half_lateral),
        pair(row1, west, west_weight),
        pair(row1, east, east_weight),
    ]
    j = lane & 3
    p = lane >> 2
    less_weight = jnp.where((p > 1) | (gx == 1), half_lateral, 0.0)
    more_weight = jnp.where((p < 8) | (gx == 0), half_lateral, 0.0)
    inner = pick(j == 1, moved(own, -1), moved(own, 1))
    outer = pick(j == 1, moved(col, 1), moved(col, -1))
    col_terms = [
        pair(col, inner, half_lateral),
        pair(col, outer, half_lateral),
        pair(col, moved(col, 4), less_weight),
        pair(col, moved(col, -4), more_weight),
    ]
    total = []
    for terms in (row_terms, col_terms):
        total.append((sum(t[0] for t in terms), sum(t[1] for t in terms)))
    return total


def first_kernel(
    y_count, z_count, h, k, e_in, r_in, g_in, rows, columns, from_even, from_odd, far_even, far_odd,
    port, t_up, t_down, w, s_up, s_down, s_w, col_raw,
    e, r, g, se, sr, sg, sk, sh, y_k, y_h, x_k, x_h,
):
    gx, gy, gz = lax.axis_index("gx"), lax.axis_index("gy"), lax.axis_index("gz")
    size = h.shape[0]
    count = size // ROWS
    is_top, is_bottom = gz == 0, gz == z_count - 1

    halo = merge_halo(gx, gy, from_even, from_odd, far_even, far_odd)
    col_raw[...] = halo
    col_h, col_s, col_c = unpack(col_raw[0:count, :])
    own_h, own_s, own_c = unpack(columns[0:count, :])

    def raw_row(place):
        return rows[place * count : (place + 1) * count, :]

    row_k, row_e = raw_retention(raw_row(0), raw_row(2), raw_row(4))
    far_k, unused = raw_retention(raw_row(1), raw_row(3), raw_row(5))
    col_k, col_e = raw_retention(col_h, col_s, col_c)
    own_k, unused2 = raw_retention(own_h, own_s, own_c)
    x_k[...] = row_k
    x_h[...] = raw_row(0)
    spread_columns(col_k, y_k, count)
    spread_columns(col_h, y_h, count)
    low = gx == 0
    near_k = jnp.where(low, k[line(ROWS - 1, count), :], k[line(0, count), :])
    near_h = jnp.where(low, h[line(ROWS - 1, count), :], h[line(0, count), :])
    (row_gain, row_in), (col_gain, col_in) = side_lateral(
        gx, gy, y_count, near_k, near_h, (row_k, raw_row(0)), (far_k, raw_row(1)), (col_k, col_h), (own_k, own_h)
    )
    source_at = jnp.where(is_top & (iota((count, LANES), 0) == DRIP), emitter_rate, 0.0)
    row_in = row_in + source_at * rows[6 * count : 6 * count + 1, :]
    col_in = col_in + source_at * col_raw[count : count + 1, :]
    se[...] = jnp.ones_like(se)
    sr[...] = jnp.zeros_like(sr)
    sk[...] = jnp.zeros_like(sk)
    sh[...] = jnp.zeros_like(sh)
    for place, (gain, inflow, k_part, h_part) in enumerate(
        ((row_gain + row_e, row_in, row_k, raw_row(0)), (col_gain + col_e, col_in, col_k, col_h))
    ):
        se[line(place, count), :] = gain
        sr[line(place, count), :] = inflow
        sk[line(place, count), :] = k_part
        sh[line(place, count), :] = h_part

    weights = edge_weights(gx, gy, y_count)

    def layer(z, above):
        gain, inflow = edge_terms(z, k[tile(z), :], h[tile(z), :], weights, (x_k, x_h, y_k, y_h))
        e[tile(z), :] = e_in[tile(z), :] + gain
        r[tile(z), :] = r_in[tile(z), :] + inflow
        g[tile(z), :] = g_in[tile(z), :]
        link, side_in, flux = vertical(z, count, sk, sh, above)
        sg[tile(z), :] = link
        sr[tile(z), :] = sr[tile(z), :] + side_in
        return flux

    each_layer(count, layer, jnp.zeros((ROWS, LANES), F32))
    reduce_block(count, ((e, r, g, t_up, t_down, w), (se, sr, sg, s_up, s_down, s_w)))
    write_port(count, port, e, r, g, k, h, ROWS, 0, is_bottom)
    write_port(count, port, se, sr, sg, sk, sh, SIDE, PLANES * ROWS, is_bottom)
    used = PLANES * (ROWS + SIDE)
    if used < PACK:
        port[used:PACK, :] = jnp.zeros((PACK - used, LANES), F32)


def second_kernel(y_count, z_count, *refs):
    own, received, refs = refs[0], refs[1:z_count], refs[z_count:]
    (
        t_up0, t_down0, w0, s_up, s_down, s_w, rows, col_raw, counts, h_in, conduct, alpha, power, m_shape, spread, se_old,
        port, t_up, t_down, w, h,
        gathered, ends, x, side_x, k, e, r, g, y_k, y_h, x_k, x_h,
    ) = refs
    gx, gy, gz = lax.axis_index("gx"), lax.axis_index("gy"), lax.axis_index("gz")
    count = h.shape[0] // ROWS
    is_top, is_bottom = gz == 0, gz == z_count - 1
    gather_ports(gz, z_count, own, received, gathered)
    side_x[at(0), :] = jnp.zeros((ROWS, LANES), F32)
    side_x[at(count - 1), :] = jnp.zeros((ROWS, LANES), F32)
    found = solve_chain(z_count, gathered, ROWS, 0)
    x[at(0), :], x[at(count - 1), :] = own_ends(gz, z_count, found, ROWS, ends)
    found = solve_chain(z_count, gathered, SIDE, PLANES * ROWS)
    side_first, side_last = own_ends(gz, z_count, found, SIDE, ends)
    side_x[0:SIDE, :] = side_first[0:SIDE, :]
    side_x[(count - 1) * ROWS : (count - 1) * ROWS + SIDE, :] = side_last[0:SIDE, :]
    substitute_block(count, ((x, t_up0, t_down0, w0), (side_x, s_up, s_down, s_w)))

    def raw_row(place):
        return rows[place * count : (place + 1) * count, :]

    row_h = raw_row(0) + side_x[line(0, count), :]
    col_h, col_s, col_c = unpack(col_raw[0:count, :])
    col_h = col_h + side_x[line(1, count), :]
    x_k[...] = raw_retention(row_h, raw_row(2), raw_row(4))[0]
    x_h[...] = row_h
    spread_columns(raw_retention(col_h, col_s, col_c)[0], y_k, count)
    spread_columns(col_h, y_h, count)

    def first(z, unused):
        here = tile(z)
        head = h_in[here, :] + x[here, :]
        h[here, :] = head
        k_value, effective, shape = retention(head, alpha[here, :], power[here, :], m_shape[here, :], conduct[here, :])
        k[here, :] = k_value
        spread_here = spread[here, :]
        cap = (storage_gain * spread_here) * (alpha[here, :] * power[here, :])
        e[here, :] = cap * shape + floor_gain
        r[here, :] = (-storage_gain * spread_here) * (effective - se_old[here, :])
        return unused

    each_layer(count, first, 0)
    weights = edge_weights(gx, gy, y_count)

    def second(z, above):
        here = tile(z)
        link, inflow, flux = vertical(z, count, k, h, above)
        gain, sideways = inner_lateral(k[here, :], h[here, :])
        edge_gain, edge_in = edge_terms(z, k[here, :], h[here, :], weights, (x_k, x_h, y_k, y_h))
        g[here, :] = link
        e[here, :] = e[here, :] + (gain + edge_gain)
        r[here, :] = r[here, :] + (inflow + sideways + edge_in)
        return flux

    each_layer(count, second, jnp.zeros((ROWS, LANES), F32))
    source = jnp.where(is_top, emitter_rate, 0.0)
    r[at(DRIP), :] = r[at(DRIP), :] + source * counts[...]
    reduce_block(count, ((e, r, g, t_up, t_down, w),))
    write_port(count, port, e, r, g, k, h, ROWS, 0, is_bottom)
    used = PLANES * ROWS
    if used < PACK:
        port[used:PACK, :] = jnp.zeros((PACK - used, LANES), F32)


def last_kernel(z_count, *refs):
    own, received, refs = refs[0], refs[1:z_count], refs[z_count:]
    t_up, t_down, w, h_in, kinds, head, water, gathered, ends, x = refs
    gz = lax.axis_index("gz")
    count = h_in.shape[0] // ROWS
    gather_ports(gz, z_count, own, received, gathered)
    found = solve_chain(z_count, gathered, ROWS, 0)
    x[at(0), :], x[at(count - 1), :] = own_ends(gz, z_count, found, ROWS, ends)
    substitute_block(count, ((x, t_up, t_down, w),))

    def layer(z, unused):
        here = tile(z)
        pressure = h_in[here, :] + x[here, :]
        alpha, power, m_shape, spread, residual = look_up(
            kinds[here, :].astype(F32), ALPHA_TABLE, POWER_TABLE, M_TABLE, SPREAD_TABLE, RESIDUAL_TABLE
        )
        head[here, :] = pressure
        water[here, :] = residual + spread * saturation(pressure, alpha, power, m_shape)
        return unused

    each_layer(count, layer, 0)


def per_device(sizes, head_old, ks_scale, soil_class, emitter_cells):
    x_count, y_count, z_count = sizes
    count, rows, lanes = head_old.shape
    assert (rows, lanes, x_count) == (ROWS, LANES, 2) and count > DRIP
    assert z_count & (z_count - 1) == 0
    size = count * ROWS

    def array(length):
        return jax.ShapeDtypeStruct((length, LANES), F32)

    def buffer(length):
        return pltpu.VMEM((length, LANES), F32)

    def call(kernel, name, outs, scratch, flops, *operands):
        return pl.pallas_call(
            kernel,
            name=name,
            out_shape=[array(length) for length in outs],
            in_specs=[pl.BlockSpec(memory_space=pltpu.VMEM)] * len(operands),
            out_specs=[pl.BlockSpec(memory_space=pltpu.VMEM)] * len(outs),
            scratch_shapes=[buffer(length) for length in scratch],
            compiler_params=pltpu.CompilerParams(vmem_limit_bytes=24 << 20),
            cost_estimate=pl.CostEstimate(flops=flops, bytes_accessed=flops, transcendentals=0),
        )(*operands)

    h, ks, kinds = (value.reshape(size, LANES) for value in (head_old, ks_scale, soil_class))
    cells = emitter_cells.reshape(1, -1)
    columns, rows_out, counts = call(
        pack_kernel, "pack", (count + ROWS, 6 * count + ROWS, ROWS), (size,), 1 << 20, h, ks, kinds, cells
    )
    even = [(y ^ 1, y) for y in range(y_count) if y ^ 1 < y_count]
    odd = [(y, y + 1) for y in range(1, y_count - 1, 2)]
    odd += [(b, a) for a, b in odd]
    swap = [(0, 1), (1, 0)]
    from_even = lax.ppermute(columns, "gy", even)
    from_odd = lax.ppermute(columns, "gy", odd)
    side_rows = lax.ppermute(rows_out, "gx", swap)
    far_even = lax.ppermute(from_even, "gx", swap)
    far_odd = lax.ppermute(from_odd, "gx", swap)
    k, e, r, g, se_old, alpha, power, m_shape, spread, conduct = call(
        local_kernel, "local", (size,) * 10, (), 4 << 20, h, ks, kinds, counts
    )
    port, t_up, t_down, w, s_up, s_down, s_w, col_raw = call(
        functools.partial(first_kernel, y_count, z_count),
        "first",
        (PACK, *(size,) * 6, count + ROWS),
        (*(size,) * 9, size, count, count),
        4 << 20,
        h, k, e, r, g, side_rows, columns, from_even, from_odd, far_even, far_odd,
    )

    def exchange(value):
        return [
            lax.ppermute(value, "gz", [(z, z ^ offset) for z in range(z_count)])
            for offset in range(1, z_count)
        ]

    port2, t_up, t_down, w, h1 = call(
        functools.partial(second_kernel, y_count, z_count),
        "second",
        (PACK, *(size,) * 4),
        (z_count * PACK, z_count * 2 * ROWS, *(size,) * 8, count, count),
        4 << 20,
        port, *exchange(port), t_up, t_down, w, s_up, s_down, s_w, side_rows, col_raw, counts, h, conduct, alpha, power, m_shape, spread, se_old,
    )
    head, water = call(
        functools.partial(last_kernel, z_count),
        "last",
        (size, size),
        (z_count * PACK, z_count * 2 * ROWS, size),
        4 << 20,
        port2, *exchange(port2), t_up, t_down, w, h1, kinds,
    )
    return head.reshape(head_old.shape), water.reshape(head_old.shape)


def solution(mesh):
    in_specs = (P("gz", "gx", "gy"), P("gz", "gx", "gy"), P("gz", "gx", "gy"), P("gx", "gy", None))
    out_specs = (P("gz", "gx", "gy"), P("gz", "gx", "gy"))
    sizes = tuple(mesh.shape[axis] for axis in ("gx", "gy", "gz"))
    return jax.shard_map(
        functools.partial(per_device, sizes),
        mesh=mesh, in_specs=in_specs, out_specs=out_specs, check_vma=False,
    )
```
